32 devices in a mesh: grp: 2 (over x), pan: 16 (over z, y, core).
Axes of the slice: x: 2, y: 2, z: 4, core: 2. Of those that a mesh axis runs over, the one named last changes fastest.
Arguments:
- pool_grads: bfloat16 [256, 8192], P(('grp', 'pan')), parts along dimension 0, may hold values from -6 to 6
- sample_idx: int32 [32, 4], P('grp'), parts along dimension 0, may hold values from 0 to 7
- basis: bfloat16 [16384, 8192], P('grp', 'pan'), parts along dimension 0, may hold values from -0.0625 to 0.0625
- rotations: bfloat16 [2, 2048, 8192], P(None, 'grp', 'pan'), parts along dimension 1, may hold values from -0.1875 to 0.1875
- jacobi_bits: int32 [8], P('grp'), parts along dimension 0, may hold values from 0 to 3, each once
Outputs:
- projected: bfloat16 [128, 8192], P('grp', 'pan'), parts along dimension 0
- scalings: float32 [16384], P(('grp', 'pan')), parts along dimension 0
- new_basis: bfloat16 [16384, 8192], P('grp', 'pan'), parts along dimension 0
The draws below stay inside these ranges and needn't reach their ends.
There are 2 independent parts, one for each index of `grp`. The reference program is written for one: setup_inputs(seed, part) draws one part's arguments, and reference() takes and returns one part's arrays. A program takes and returns all parts, laid end to end along the dimension named above; each array names one. Nothing has to cross between parts.
Inputs may be any that keep to these rules, and one draw needn't show every extreme that they name: `jacobi_bits`: each of the 4 bits appears once.
All inputs are finite; a program needn't handle non-finite values.
Results may differ from the reference program's by a relative error of at most 0.0057.
Values may be sent and summed in bfloat16 or wider, within the bound.
No kernel may reach another device: no remote copies, remote signals or barrier semaphores. Data moves between devices by JAX's collectives and lax.ppermute only.
A program may use at most 128 MiB of HBM per device.

```python
import jax
import jax.numpy as jnp

D = 8192
STEPS = 2
S_DEV = 4
ROWS_DEV = 8
PANEL = 512
BITS = 4
ROWS = 128
N_PAN = 16


def touch_ends(values, own_key, smallest, largest):
    longest = values.shape.index(max(values.shape))
    spots = []
    for shift in (0, 1):
        where = [jax.random.randint(jax.random.fold_in(own_key, axis), (), 0, length) for axis, length in enumerate(values.shape)]
        where[longest] = (where[longest] + shift) % values.shape[longest]
        spots.append(tuple(where))
    return values.at[spots[0]].set(smallest).at[spots[1]].set(largest)


def levels(stream_key, dims, shards, smallest, largest):
    loudness, own = 1.0, jax.random.fold_in(stream_key, 6)
    for dim, parts in shards:
        heights = jnp.exp(jax.random.uniform(jax.random.fold_in(own, dim), (parts,), jnp.float32, smallest / len(shards), largest / len(shards)))
        loudness = loudness * jnp.repeat(heights, dims[dim] // parts).reshape([-1 if axis == dim else 1 for axis in range(len(dims))])
    return loudness


def normal_values(own_key, extent, scale, reach, shards=(), held_as=jnp.bfloat16):
    gain = levels(own_key, extent, shards, -0.22, 0.18) if shards else 1.0
    drawn = jax.random.normal(own_key, extent, jnp.float32) * scale * gain
    return jnp.minimum(jnp.maximum(drawn, -reach), reach).astype(held_as)


def setup_inputs(seed: int = 0, part: int = 0) -> dict:
    streams_of = jax.random.split(jax.random.key(seed), 6)
    part_splits = jax.random.split(jax.random.fold_in(streams_of[5], part), 6)
    return {
        "pool_grads": normal_values(part_splits[0], (ROWS, D), 1.0, 6.0, ((0, 16),)),
        "sample_idx": touch_ends(jax.random.randint(part_splits[1], (N_PAN, S_DEV), 0, ROWS_DEV), jax.random.fold_in(part_splits[1], 1), 0, ROWS_DEV - 1).astype(jnp.int32),
        "basis": normal_values(part_splits[2], (D, D), D ** -0.5, 0.0625, ((1, 16),)),
        "rotations": normal_values(part_splits[3], (STEPS, 2 * PANEL, D), (2 * PANEL) ** -0.5, 0.1875, ((2, 16),)),
        "jacobi_bits": jax.random.permutation(part_splits[4], BITS).astype(jnp.int32),
    }


def reference(pool_grads, sample_idx, basis, rotations, jacobi_bits):
    count = N_PAN
    width = PANEL
    offsets = jnp.arange(count, dtype=jnp.int32)[:, None] * ROWS_DEV
    flat_idx = (offsets + sample_idx.astype(jnp.int32)).reshape(-1)
    samples = jnp.take(pool_grads, flat_idx, axis=0)
    panels = jnp.arange(count, dtype=jnp.int32)
    current = basis
    for step in range(STEPS):
        shift_bit = jnp.left_shift(jnp.int32(1), jacobi_bits[step].astype(jnp.int32))
        partner = jnp.bitwise_xor(panels, shift_bit)
        blocks = current.reshape(D, count, width)
        other = jnp.take(blocks, partner, axis=1)
        rotate = rotations[step].reshape(2 * width, count, width).astype(jnp.float32)
        fresh = jnp.einsum("dnp,pnq->dnq", blocks.astype(jnp.float32), rotate[:width])
        fresh = fresh + jnp.einsum("dnp,pnq->dnq", other.astype(jnp.float32), rotate[width:])
        current = fresh.reshape(D, D).astype(jnp.bfloat16)
    full = jnp.dot(samples, current, preferred_element_type=jnp.float32)
    return full.astype(jnp.bfloat16), jnp.mean(full * full, axis=0), current
```

```python
from functools import partial

import jax
import jax.numpy as jnp
from jax import lax
from jax.experimental import pallas as pl
from jax.experimental.pallas import tpu as pltpu
from jax.sharding import PartitionSpec as P

CHUNK_BYTES = 1 << 20
TILE = 256


def swapped(x, bit):
    return lax.ppermute(x, "pan", [(i, i ^ 1 << bit) for i in range(lax.axis_size("pan"))])


def gather_samples(own):
    picked, columns = own.shape
    rows = own[None]
    for bit in reversed(range(lax.axis_size("pan").bit_length() - 1)):
        rows = jnp.concatenate([rows, swapped(rows, bit)])
    return rows.reshape(-1, columns)


def in_device_order(values, picked):
    me, count = lax.axis_index("pan"), lax.axis_size("pan")
    order = [0]
    for bit in reversed(range(count.bit_length() - 1)):
        order += [held ^ 1 << bit for held in order]
    source = jnp.array(order, jnp.int32) ^ me
    rows = (source[:, None] * picked + jnp.arange(picked, dtype=jnp.int32)).reshape(-1)
    pick = (jnp.arange(values.shape[0], dtype=jnp.int32)[:, None] == rows[None, :]).astype(values.dtype)
    return jnp.dot(pick, values, preferred_element_type=jnp.float32).astype(values.dtype)


def rotate(own, own_chunk, other, rotations, step, rows):
    width = own.shape[1]
    tile = min(TILE, rows)
    first = own_chunk * (rows // tile)

    def kernel(own_ref, other_ref, map_ref, fresh_ref):
        fresh = jnp.dot(own_ref[...], map_ref[:width], preferred_element_type=jnp.float32)
        fresh = fresh + jnp.dot(other_ref[...], map_ref[width:], preferred_element_type=jnp.float32)
        fresh_ref[...] = fresh.astype(jnp.bfloat16)

    return pl.pallas_call(
        kernel,
        grid=(rows // tile,),
        in_specs=[
            pl.BlockSpec((tile, width), lambda i: (first + i, 0)),
            pl.BlockSpec((tile, width), lambda i: (i, 0)),
            pl.BlockSpec((None, 2 * width, width), lambda i: (step, 0, 0)),
        ],
        out_specs=pl.BlockSpec((tile, width), lambda i: (i, 0)),
        out_shape=jax.ShapeDtypeStruct((rows, width), jnp.bfloat16),
        cost_estimate=pl.CostEstimate(
            flops=4 * rows * width * width, bytes_accessed=6 * rows * width + 4 * width * width, transcendentals=0
        ),
    )(own, other, rotations)


def finish(own, other, rotations, step, samples, full, basis_out, chunk, depth):
    rows, width = own.shape
    tile = min(TILE, rows)
    first = chunk * (rows // tile)
    count = samples.shape[0]
    start = full is None

    def kernel(*refs):
        own_ref, other_ref, map_ref, samples_ref = refs[:4]
        fresh_ref, sum_ref = refs[-2:]
        fresh = jnp.dot(own_ref[...], map_ref[:width], preferred_element_type=jnp.float32)
        fresh = fresh + jnp.dot(other_ref[...], map_ref[width:], preferred_element_type=jnp.float32)
        fresh = fresh.astype(jnp.bfloat16)
        fresh_ref[...] = fresh

        @pl.when(pl.program_id(0) == 0)
        def _():
            sum_ref[...] = jnp.zeros_like(sum_ref) if start else refs[4][...]

        sum_ref[...] += jnp.dot(samples_ref[...], fresh, preferred_element_type=jnp.float32)

    in_specs = [
        pl.BlockSpec((tile, width), lambda i: (i, 0)),
        pl.BlockSpec((tile, width), lambda i: (i, 0)),
        pl.BlockSpec((None, 2 * width, width), lambda i: (step, 0, 0)),
        pl.BlockSpec((count, tile), lambda i: (0, first + i)),
    ]
    args = [own, other, rotations, samples]
    aliases = {}
    if not start:
        in_specs += [pl.BlockSpec((count, width), lambda i: (0, 0)), pl.BlockSpec(memory_space=pl.ANY)]
        args += [full, basis_out]
        aliases = {5: 0}
    basis_out, full = pl.pallas_call(
        kernel,
        grid=(rows // tile,),
        in_specs=in_specs,
        out_specs=[
            pl.BlockSpec((tile, width), lambda i: (first + i, 0)),
            pl.BlockSpec((count, width), lambda i: (0, 0)),
        ],
        out_shape=[
            jax.ShapeDtypeStruct((depth, width), jnp.bfloat16),
            jax.ShapeDtypeStruct((count, width), jnp.float32),
        ],
        input_output_aliases=aliases,
        cost_estimate=pl.CostEstimate(
            flops=4 * rows * width * width + 2 * count * rows * width,
            bytes_accessed=6 * rows * width + 4 * width * width + 2 * count * rows,
            transcendentals=0,
        ),
    )(*args)
    return full, basis_out


def refresh(own, basis, rotations, bits):
    depth, width = basis.shape
    chunks = max(1, depth * width * 2 // CHUNK_BYTES)
    size = depth // chunks
    samples = gather_samples(own)
    full, basis_out = None, None
    for chunk in range(chunks):
        other = swapped(basis[chunk * size : (chunk + 1) * size], bits[0])
        middle = rotate(basis, chunk, other, rotations, 0, size)
        other = swapped(middle, bits[1])
        full, basis_out = finish(middle, other, rotations, 1, samples, full, basis_out, chunk, depth)
    return full, basis_out


def body(pool_grads, sample_idx, basis, rotations, jacobi_bits):
    bit_count = lax.axis_size("pan").bit_length() - 1
    own = jnp.take(pool_grads, sample_idx[lax.axis_index("pan")], axis=0)
    pairs = [(a, b) for a in range(bit_count) for b in range(bit_count) if a != b]
    first, second = jacobi_bits[0], jacobi_bits[1]
    branch = first * (bit_count - 1) + second - (second > first).astype(jnp.int32)
    full, current = lax.switch(branch, [partial(refresh, bits=pair) for pair in pairs], own, basis, rotations)
    projected = in_device_order(full.astype(jnp.bfloat16), own.shape[0])
    return (projected, jnp.mean(full * full, axis=0), current)


def solution(mesh):
    in_specs = (
        P(("grp", "pan"), None),
        P("grp", None),
        P("grp", "pan"),
        P(None, "grp", "pan"),
        P("grp"),
    )
    out_specs = (P("grp", "pan"), P(("grp", "pan")), P("grp", "pan"))
    return jax.shard_map(body, mesh=mesh, in_specs=in_specs, out_specs=out_specs, check_vma=False)
```

```python
from functools import partial

import jax
import jax.numpy as jnp
from jax import lax
from jax.experimental import pallas as pl
from jax.experimental.pallas import tpu as pltpu
from jax.sharding import PartitionSpec as P

UNITS = 16
TILE = 128
HBM = pl.BlockSpec(memory_space=pltpu.HBM)


def plan(bits, width):
    if width < 256:
        return [8, 8]
    near = {0: 0, 1: 2, 2: 2}
    first, second = near.get(bits[0], 4), near.get(bits[1], 4)
    if 0 in (first, second):
        sizes = [2, 4, 5, 5]
    elif first != second:
        sizes = [1, 2, 3, 3, 3, 4]
    else:
        return [2] * 8
    return sizes if first < second else sizes[::-1]


def swapped(x, bit):
    return lax.ppermute(x, "pan", [(i, i ^ 1 << bit) for i in range(lax.axis_size("pan"))])


def after(x, *earlier):
    return lax.optimization_barrier((x, *earlier))[0]


def in_device_order(values, picked):
    me, count = lax.axis_index("pan"), lax.axis_size("pan")
    order = [0]
    for bit in reversed(range(count.bit_length() - 1)):
        order += [held ^ 1 << bit for held in order]
    source = jnp.array(order, jnp.int32) ^ me
    rows = (source[:, None] * picked + jnp.arange(picked, dtype=jnp.int32)).reshape(-1)
    pick = (jnp.arange(values.shape[0], dtype=jnp.int32)[:, None] == rows[None, :]).astype(values.dtype)
    return jnp.dot(pick, values, preferred_element_type=jnp.float32).astype(values.dtype)


def cost(rows, width, columns):
    return pl.CostEstimate(
        flops=2 * rows * width * columns, bytes_accessed=2 * (rows * width + width * columns + rows * columns), transcendentals=0
    )


def rotate(own, own_start, other, rotations, step, whole=None, start=0, depth=None):
    rows, width = other.shape
    tiles = rows // TILE

    def kernel(own_ref, other_ref, maps_ref, *rest):
        fresh_ref, own_held, other_held, map_held, fresh_held, map_sem, in_sems, out_sem = rest[-8:]

        def arrivals(i):
            at = pl.ds(pl.multiple_of(i * TILE, TILE), TILE)
            source = pl.ds(pl.multiple_of(own_start + i * TILE, TILE), TILE)
            return [
                pltpu.make_async_copy(own_ref.at[source], own_held.at[at], in_sems.at[0, i]),
                pltpu.make_async_copy(other_ref.at[at], other_held.at[at], in_sems.at[1, i]),
            ]

        def fetch(i, carry):
            for copy in arrivals(i):
                copy.start()
            return carry

        def tile(i, carry):
            for copy in arrivals(i):
                copy.wait()
            at = pl.ds(pl.multiple_of(i * TILE, TILE), TILE)
            target = pl.ds(pl.multiple_of(start + i * TILE, TILE), TILE)
            pair = jnp.concatenate([own_held[at], other_held[at]], axis=1)
            fresh = jnp.dot(pair, map_held[...], preferred_element_type=jnp.float32)
            fresh_held[at] = fresh.astype(jnp.bfloat16)
            pltpu.make_async_copy(fresh_held.at[at], fresh_ref.at[target], out_sem).start()
            return carry

        map_copy = pltpu.make_async_copy(maps_ref.at[step], map_held, map_sem)
        map_copy.start()
        lax.fori_loop(0, tiles, fetch, 0)
        map_copy.wait()
        lax.fori_loop(0, tiles, tile, 0)
        pltpu.make_async_copy(fresh_held, fresh_ref.at[pl.ds(start, rows)], out_sem).wait()

    args = [own, other, rotations] + [whole] * (whole is not None)
    return pl.pallas_call(
        kernel,
        in_specs=[HBM] * len(args),
        out_specs=HBM,
        out_shape=jax.ShapeDtypeStruct((depth or rows, width), jnp.bfloat16),
        scratch_shapes=[
            pltpu.VMEM((rows, width), jnp.bfloat16),
            pltpu.VMEM((rows, width), jnp.bfloat16),
            pltpu.VMEM((2 * width, width), jnp.bfloat16),
            pltpu.VMEM((rows, width), jnp.bfloat16),
            pltpu.SemaphoreType.DMA,
            pltpu.SemaphoreType.DMA((2, tiles)),
            pltpu.SemaphoreType.DMA,
        ],
        input_output_aliases={} if whole is None else {3: 0},
        compiler_params=pltpu.CompilerParams(vmem_limit_bytes=60 << 20),
        cost_estimate=cost(rows, 2 * width, width),
    )(*args)


def project(samples, basis, start, rows, full=None):
    width = basis.shape[1]
    count = samples.shape[0]
    tile = depth_tile(start, rows)
    first = start // tile

    def kernel(samples_ref, basis_ref, *rest):
        sum_ref = rest[-1]

        @pl.when(pl.program_id(0) == 0)
        def _():
            sum_ref[...] = jnp.zeros_like(sum_ref) if full is None else rest[0][...]

        sum_ref[...] += jnp.dot(samples_ref[...], basis_ref[...], preferred_element_type=jnp.float32)

    held = pl.BlockSpec((count, width), lambda i: (0, 0))
    return pl.pallas_call(
        kernel,
        grid=(rows // tile,),
        in_specs=[
            pl.BlockSpec((count, tile), lambda i: (0, first + i)),
            pl.BlockSpec((tile, width), lambda i: (first + i, 0)),
        ]
        + [held] * (full is not None),
        out_specs=held,
        out_shape=jax.ShapeDtypeStruct((count, width), jnp.float32),
        compiler_params=pltpu.CompilerParams(vmem_limit_bytes=60 << 20),
        cost_estimate=cost(count, rows, width),
    )(*([samples, basis] + [full] * (full is not None)))


def depth_tile(start, rows):
    tile = 512
    while start % tile or rows % tile:
        tile //= 2
    return tile


def joined(upper, lower):
    count = upper.shape[0]

    def kernel(upper_ref, lower_ref, whole_ref, sems):
        copies = [
            pltpu.make_async_copy(upper_ref, whole_ref.at[:count], sems.at[0]),
            pltpu.make_async_copy(lower_ref, whole_ref.at[count:], sems.at[1]),
        ]
        for copy in copies:
            copy.start()
        for copy in copies:
            copy.wait()

    return pl.pallas_call(
        kernel,
        in_specs=[HBM, HBM],
        out_specs=HBM,
        out_shape=jax.ShapeDtypeStruct((2 * count, *upper.shape[1:]), upper.dtype),
        scratch_shapes=[pltpu.SemaphoreType.DMA((2,))],
        compiler_params=pltpu.CompilerParams(vmem_limit_bytes=60 << 20),
        cost_estimate=pl.CostEstimate(flops=0, bytes_accessed=8 * upper.size, transcendentals=0),
    )(upper, lower)


def refresh(own, basis, rotations, bits):
    depth, width = basis.shape
    sizes = [units * depth // UNITS for units in plan(bits, width)]
    starts = [sum(sizes[:i]) for i in range(len(sizes))]
    chunks = len(sizes)
    picked, columns = own.shape
    gather_bits = list(reversed(range(lax.axis_size("pan").bit_length() - 1)))

    def send(chunk, *earlier):
        return swapped(after(basis, *earlier)[starts[chunk] : starts[chunk] + sizes[chunk]], bits[0])

    join_stages = [min(2 * i, chunks - 1) for i in range(1, len(gather_bits))]
    samples = own[None]
    sent = swapped(samples, gather_bits.pop(0))
    arriving = [send(0)]
    samples = joined(samples, sent)
    sent = swapped(samples, gather_bits.pop(0))
    arriving.append(send(1, samples))
    basis_out = middle = other = full = None
    for chunk in range(chunks):
        held = basis
        while join_stages and join_stages[0] == chunk and gather_bits:
            join_stages.pop(0)
            samples = joined(samples, sent)
            sent = swapped(samples, gather_bits.pop(0))
            held = after(basis, samples)
        fresh = rotate(held, starts[chunk], arriving[chunk], rotations, 0)
        coming = swapped(fresh, bits[1])
        if chunk + 2 < chunks:
            arriving.append(send(chunk + 2, fresh))
        if chunk > 0:
            basis_out = rotate(after(middle, fresh), 0, other, rotations, 1, basis_out, starts[chunk - 1], depth)
            if chunk + 1 < chunks:
                arriving[chunk + 1] = after(arriving[chunk + 1], basis_out)
        middle, other = fresh, coming
    while sent is not None:
        samples = joined(samples, sent)
        sent = swapped(samples, gather_bits.pop(0)) if gather_bits else None
    samples = samples.reshape(-1, columns)
    full = project(samples, basis_out, 0, starts[-1])
    basis_out = rotate(after(middle, full), 0, other, rotations, 1, basis_out, starts[-1], depth)
    full = project(samples, basis_out, starts[-1], sizes[-1], full)
    return full, basis_out


def body(pool_grads, sample_idx, basis, rotations, jacobi_bits):
    bit_count = lax.axis_size("pan").bit_length() - 1
    own = jnp.take(pool_grads, sample_idx[lax.axis_index("pan")], axis=0)
    pairs = [(a, b) for a in range(bit_count) for b in range(bit_count) if a != b]
    first, second = jacobi_bits[0], jacobi_bits[1]
    branch = first * (bit_count - 1) + second - (second > first).astype(jnp.int32)
    full, current = lax.switch(branch, [partial(refresh, bits=pair) for pair in pairs], own, basis, rotations)
    projected = in_device_order(full.astype(jnp.bfloat16), own.shape[0])
    return (projected, jnp.mean(full * full, axis=0), current)


def solution(mesh):
    in_specs = (
        P(("grp", "pan"), None),
        P("grp", None),
        P("grp", "pan"),
        P(None, "grp", "pan"),
        P("grp"),
    )
    out_specs = (P("grp", "pan"), P(("grp", "pan")), P("grp", "pan"))
    return jax.shard_map(body, mesh=mesh, in_specs=in_specs, out_specs=out_specs, check_vma=False)
```

```python
from functools import partial

import jax
import jax.numpy as jnp
from jax import lax
from jax.experimental import pallas as pl
from jax.experimental.pallas import tpu as pltpu
from jax.sharding import PartitionSpec as P

UNITS = 16
TILE = 128
HBM = pl.BlockSpec(memory_space=pltpu.HBM)


def plan(bits, width):
    if width < 256:
        return [8, 8]
    near = {0: 0, 1: 2, 2: 2}
    first, second = near.get(bits[0], 4), near.get(bits[1], 4)
    if 0 in (first, second):
        sizes = [2, 4, 5, 5]
    elif first != second:
        sizes = [1, 2, 3, 3, 3, 4]
    else:
        return [2] * 8
    return sizes if first < second else sizes[::-1]


def swapped(x, bit):
    return lax.ppermute(x, "pan", [(i, i ^ 1 << bit) for i in range(lax.axis_size("pan"))])


def after(x, *earlier):
    return lax.optimization_barrier((x, *earlier))[0]


def in_device_order(values, picked):
    me, count = lax.axis_index("pan"), lax.axis_size("pan")
    order = [0]
    for bit in reversed(range(count.bit_length() - 1)):
        order += [held ^ 1 << bit for held in order]
    source = jnp.array(order, jnp.int32) ^ me
    rows = (source[:, None] * picked + jnp.arange(picked, dtype=jnp.int32)).reshape(-1)
    pick = (jnp.arange(values.shape[0], dtype=jnp.int32)[:, None] == rows[None, :]).astype(values.dtype)
    return jnp.dot(pick, values, preferred_element_type=jnp.float32).astype(values.dtype)


def cost(rows, width, columns):
    return pl.CostEstimate(
        flops=2 * rows * width * columns, bytes_accessed=2 * (rows * width + width * columns + rows * columns), transcendentals=0
    )


def rotate(own, own_start, other, rotations, step, whole=None, start=0, depth=None):
    rows, width = other.shape
    tiles = rows // TILE

    def kernel(own_ref, other_ref, maps_ref, *rest):
        fresh_ref, own_held, other_held, map_held, fresh_held, map_sem, in_sems, out_sem = rest[-8:]

        def arrivals(i):
            at = pl.ds(pl.multiple_of(i * TILE, TILE), TILE)
            source = pl.ds(pl.multiple_of(own_start + i * TILE, TILE), TILE)
            return [
                pltpu.make_async_copy(own_ref.at[source], own_held.at[at], in_sems.at[0, i]),
                pltpu.make_async_copy(other_ref.at[at], other_held.at[at], in_sems.at[1, i]),
            ]

        def fetch(i, carry):
            for copy in arrivals(i):
                copy.start()
            return carry

        def tile(i, carry):
            for copy in arrivals(i):
                copy.wait()
            at = pl.ds(pl.multiple_of(i * TILE, TILE), TILE)
            target = pl.ds(pl.multiple_of(start + i * TILE, TILE), TILE)
            pair = jnp.concatenate([own_held[at], other_held[at]], axis=1)
            fresh = jnp.dot(pair, map_held[...], preferred_element_type=jnp.float32)
            fresh_held[at] = fresh.astype(jnp.bfloat16)
            pltpu.make_async_copy(fresh_held.at[at], fresh_ref.at[target], out_sem).start()
            return carry

        map_copy = pltpu.make_async_copy(maps_ref.at[step], map_held, map_sem)
        map_copy.start()
        lax.fori_loop(0, tiles, fetch, 0)
        map_copy.wait()
        lax.fori_loop(0, tiles, tile, 0)
        pltpu.make_async_copy(fresh_held, fresh_ref.at[pl.ds(start, rows)], out_sem).wait()

    args = [own, other, rotations] + [whole] * (whole is not None)
    return pl.pallas_call(
        kernel,
        in_specs=[HBM] * len(args),
        out_specs=HBM,
        out_shape=jax.ShapeDtypeStruct((depth or rows, width), jnp.bfloat16),
        scratch_shapes=[
            pltpu.VMEM((rows, width), jnp.bfloat16),
            pltpu.VMEM((rows, width), jnp.bfloat16),
            pltpu.VMEM((2 * width, width), jnp.bfloat16),
            pltpu.VMEM((rows, width), jnp.bfloat16),
            pltpu.SemaphoreType.DMA,
            pltpu.SemaphoreType.DMA((2, tiles)),
            pltpu.SemaphoreType.DMA,
        ],
        input_output_aliases={} if whole is None else {3: 0},
        compiler_params=pltpu.CompilerParams(vmem_limit_bytes=60 << 20),
        cost_estimate=cost(rows, 2 * width, width),
    )(*args)


def project(samples, basis, start, rows, full=None):
    width = basis.shape[1]
    count = samples.shape[0]
    tile = depth_tile(start, rows)
    first = start // tile

    def kernel(samples_ref, basis_ref, *rest):
        sum_ref = rest[-1]

        @pl.when(pl.program_id(0) == 0)
        def _():
            sum_ref[...] = jnp.zeros_like(sum_ref) if full is None else rest[0][...]

        sum_ref[...] += jnp.dot(samples_ref[...], basis_ref[...], preferred_element_type=jnp.float32)

    held = pl.BlockSpec((count, width), lambda i: (0, 0))
    return pl.pallas_call(
        kernel,
        grid=(rows // tile,),
        in_specs=[
            pl.BlockSpec((count, tile), lambda i: (0, first + i)),
            pl.BlockSpec((tile, width), lambda i: (first + i, 0)),
        ]
        + [held] * (full is not None),
        out_specs=held,
        out_shape=jax.ShapeDtypeStruct((count, width), jnp.float32),
        compiler_params=pltpu.CompilerParams(vmem_limit_bytes=60 << 20),
        cost_estimate=cost(count, rows, width),
    )(*([samples, basis] + [full] * (full is not None)))


def depth_tile(start, rows):
    tile = 512
    while start % tile or rows % tile:
        tile //= 2
    return tile


def gather_samples(own):
    picked, columns = own.shape
    rows = own[None]
    for bit in reversed(range(lax.axis_size("pan").bit_length() - 1)):
        rows = jnp.concatenate([rows, swapped(rows, bit)])
    return rows.reshape(-1, columns)


def refresh(samples, basis, rotations, bits):
    depth, width = basis.shape
    sizes = [units * depth // UNITS for units in plan(bits, width)]
    starts = [sum(sizes[:i]) for i in range(len(sizes))]
    chunks = len(sizes)

    def send(chunk, *earlier):
        return swapped(after(basis, *earlier)[starts[chunk] : starts[chunk] + sizes[chunk]], bits[0])

    arriving = [send(0), send(1)]
    basis_out = middle = other = None
    for chunk in range(chunks):
        fresh = rotate(basis, starts[chunk], arriving[chunk], rotations, 0)
        coming = swapped(fresh, bits[1])
        if chunk + 2 < chunks:
            arriving.append(send(chunk + 2, fresh))
        if chunk > 0:
            basis_out = rotate(after(middle, fresh), 0, other, rotations, 1, basis_out, starts[chunk - 1], depth)
            if chunk + 1 < chunks:
                arriving[chunk + 1] = after(arriving[chunk + 1], basis_out)
        middle, other = fresh, coming
    full = project(samples, basis_out, 0, starts[-1])
    basis_out = rotate(after(middle, full), 0, other, rotations, 1, basis_out, starts[-1], depth)
    full = project(samples, basis_out, starts[-1], sizes[-1], full)
    return full, basis_out


def body(pool_grads, sample_idx, basis, rotations, jacobi_bits):
    bit_count = lax.axis_size("pan").bit_length() - 1
    own = jnp.take(pool_grads, sample_idx[lax.axis_index("pan")], axis=0)
    samples = gather_samples(own)
    pairs = [(a, b) for a in range(bit_count) for b in range(bit_count) if a != b]
    first, second = jacobi_bits[0], jacobi_bits[1]
    branch = first * (bit_count - 1) + second - (second > first).astype(jnp.int32)
    full, current = lax.switch(branch, [partial(refresh, bits=pair) for pair in pairs], samples, basis, rotations)
    projected = in_device_order(full.astype(jnp.bfloat16), own.shape[0])
    return (projected, jnp.mean(full * full, axis=0), current)


def solution(mesh):
    in_specs = (
        P(("grp", "pan"), None),
        P("grp", None),
        P("grp", "pan"),
        P(None, "grp", "pan"),
        P("grp"),
    )
    out_specs = (P("grp", "pan"), P(("grp", "pan")), P("grp", "pan"))
    return jax.shard_map(body, mesh=mesh, in_specs=in_specs, out_specs=out_specs, check_vma=False)
```

```python
from functools import partial

import jax
import jax.numpy as jnp
from jax import lax
from jax.experimental import pallas as pl
from jax.experimental.pallas import tpu as pltpu
from jax.sharding import PartitionSpec as P

UNITS = 32
TILE = 128
SHARE = 1024
HBM = pl.BlockSpec(memory_space=pltpu.HBM)


def plan(bits, width):
    if width < 256:
        return [16, 16], 2, "MMFFP"
    near = {0: 0, 1: 2, 2: 2}
    first, second = near.get(bits[0], 4), near.get(bits[1], 4)
    if second == 0:
        return [12, 10, 7, 3], 2, "MMFMFPMFFP"
    if first == 0:
        return [8] * 4, 4, "MMMMFFFPFP"
    if first > second:
        return [8, 8, 7, 4, 3, 2], 2, "MMFMFMFMFPMFFP"
    if first < second:
        return [4] * 8, 8, "MMMMFMFMFMFMFFFPFP"
    return [4] * 8, 2, "MM" + "FM" * 6 + "FPFP"


def swapped(x, bit):
    return lax.ppermute(x, "pan", [(i, i ^ 1 << bit) for i in range(lax.axis_size("pan"))])


def after(x, *earlier):
    return lax.optimization_barrier((x, *earlier))[0]


def in_device_order(values, picked):
    me, count = lax.axis_index("pan"), lax.axis_size("pan")
    order = [0]
    for bit in reversed(range(count.bit_length() - 1)):
        order += [held ^ 1 << bit for held in order]
    source = jnp.array(order, jnp.int32) ^ me
    rows = (source[:, None] * picked + jnp.arange(picked, dtype=jnp.int32)).reshape(-1)
    pick = (jnp.arange(values.shape[0], dtype=jnp.int32)[:, None] == rows[None, :]).astype(values.dtype)
    return jnp.dot(pick, values, preferred_element_type=jnp.float32).astype(values.dtype)


def cost(rows, width, columns):
    return pl.CostEstimate(
        flops=rows * width * columns // SHARE, bytes_accessed=rows * (width + columns) // SHARE, transcendentals=0
    )


def rotate(own, own_start, other, rotations, step, whole=None, start=0, depth=None):
    rows, width = other.shape
    tiles = rows // TILE

    def kernel(own_ref, other_ref, maps_ref, *rest):
        fresh_ref, own_held, other_held, map_held, fresh_held, map_sem, in_sems, out_sem = rest[-8:]

        def arrivals(i):
            at = pl.ds(pl.multiple_of(i * TILE, TILE), TILE)
            source = pl.ds(pl.multiple_of(own_start + i * TILE, TILE), TILE)
            return [
                pltpu.make_async_copy(own_ref.at[source], own_held.at[at], in_sems.at[0, i]),
                pltpu.make_async_copy(other_ref.at[at], other_held.at[at], in_sems.at[1, i]),
            ]

        def fetch(i, carry):
            for copy in arrivals(i):
                copy.start()
            return carry

        def tile(i, carry):
            for copy in arrivals(i):
                copy.wait()
            at = pl.ds(pl.multiple_of(i * TILE, TILE), TILE)
            target = pl.ds(pl.multiple_of(start + i * TILE, TILE), TILE)
            pair = jnp.concatenate([own_held[at], other_held[at]], axis=1)
            fresh = jnp.dot(pair, map_held[...], preferred_element_type=jnp.float32)
            fresh_held[at] = fresh.astype(jnp.bfloat16)
            pltpu.make_async_copy(fresh_held.at[at], fresh_ref.at[target], out_sem).start()
            return carry

        map_copy = pltpu.make_async_copy(maps_ref.at[step], map_held, map_sem)
        map_copy.start()
        lax.fori_loop(0, tiles, fetch, 0)
        map_copy.wait()
        lax.fori_loop(0, tiles, tile, 0)
        pltpu.make_async_copy(fresh_held, fresh_ref.at[pl.ds(start, rows)], out_sem).wait()

    args = [own, other, rotations] + [whole] * (whole is not None)
    return pl.pallas_call(
        kernel,
        in_specs=[HBM] * len(args),
        out_specs=HBM,
        out_shape=jax.ShapeDtypeStruct((depth or rows, width), jnp.bfloat16),
        scratch_shapes=[
            pltpu.VMEM((rows, width), jnp.bfloat16),
            pltpu.VMEM((rows, width), jnp.bfloat16),
            pltpu.VMEM((2 * width, width), jnp.bfloat16),
            pltpu.VMEM((rows, width), jnp.bfloat16),
            pltpu.SemaphoreType.DMA,
            pltpu.SemaphoreType.DMA((2, tiles)),
            pltpu.SemaphoreType.DMA,
        ],
        input_output_aliases={} if whole is None else {3: 0},
        compiler_params=pltpu.CompilerParams(vmem_limit_bytes=60 << 20),
        cost_estimate=cost(rows, 2 * width, width),
    )(*args)


def project(samples, basis, start, rows, full=None):
    width = basis.shape[1]
    count = samples.shape[0]
    tile = min(1024, rows)
    depth = min(512, tile)
    first = start // tile

    def kernel(samples_ref, basis_ref, *rest):
        sum_ref = rest[-1]

        @pl.when(pl.program_id(0) == 0)
        def _():
            sum_ref[...] = jnp.zeros_like(sum_ref) if full is None else rest[0][...]

        def part(j, carry):
            at = pl.ds(pl.multiple_of(j * depth, depth), depth)
            sum_ref[...] += jnp.dot(samples_ref[:, at], basis_ref[at], preferred_element_type=jnp.float32)
            return carry

        lax.fori_loop(0, tile // depth, part, 0)

    held = pl.BlockSpec((count, width), lambda i: (0, 0))
    return pl.pallas_call(
        kernel,
        grid=(rows // tile,),
        in_specs=[
            pl.BlockSpec((count, tile), lambda i: (0, first + i)),
            pl.BlockSpec((tile, width), lambda i: (first + i, 0)),
        ]
        + [held] * (full is not None),
        out_specs=held,
        out_shape=jax.ShapeDtypeStruct((count, width), jnp.float32),
        compiler_params=pltpu.CompilerParams(vmem_limit_bytes=60 << 20),
        cost_estimate=cost(count, rows, width),
    )(*([samples, basis] + [full] * (full is not None)))


def gather_samples(own):
    picked, columns = own.shape
    rows = own[None]
    for bit in reversed(range(lax.axis_size("pan").bit_length() - 1)):
        rows = jnp.concatenate([rows, swapped(rows, bit)])
    return rows.reshape(-1, columns)


def refresh(samples, basis, rotations, bits):
    depth, width = basis.shape
    units, window, order = plan(bits, width)
    sizes = [part * depth // UNITS for part in units]
    starts = [sum(sizes[:i]) for i in range(len(sizes))]
    chunks = len(sizes)

    def send(chunk, *earlier):
        return swapped(after(basis, *earlier)[starts[chunk] : starts[chunk] + sizes[chunk]], bits[0])

    arriving = [send(0)]
    for chunk in range(1, min(window, chunks)):
        arriving.append(send(chunk, *arriving[: sizes[chunk] > sizes[chunk - 1]]))
    middles, coming = [], []
    basis_out = full = None
    done = projected = 0
    earlier = ()
    for kind in order:
        if kind == "M":
            chunk = len(middles)
            fresh = rotate(after(basis, *earlier), starts[chunk], arriving[chunk], rotations, 0)
            middles.append(fresh)
            coming.append(swapped(fresh, bits[1]))
            if chunk + window < chunks:
                arriving.append(send(chunk + window, fresh))
            earlier = (fresh,)
        elif kind == "F":
            basis_out = rotate(after(middles[done], *earlier), 0, coming[done], rotations, 1, basis_out, starts[done], depth)
            done += 1
            earlier = (basis_out,)
        else:
            end = starts[done] // 1024 * 1024 if done < chunks else depth
            full = project(after(samples, *earlier), basis_out, projected, end - projected, full)
            projected = end
            earlier = (full,)
    return full, basis_out


def body(pool_grads, sample_idx, basis, rotations, jacobi_bits):
    bit_count = lax.axis_size("pan").bit_length() - 1
    own = jnp.take(pool_grads, sample_idx[lax.axis_index("pan")], axis=0)
    samples = gather_samples(own)
    pairs = [(a, b) for a in range(bit_count) for b in range(bit_count) if a != b]
    first, second = jacobi_bits[0], jacobi_bits[1]
    branch = first * (bit_count - 1) + second - (second > first).astype(jnp.int32)
    full, current = lax.switch(branch, [partial(refresh, bits=pair) for pair in pairs], samples, basis, rotations)
    projected = in_device_order(full.astype(jnp.bfloat16), own.shape[0])
    return (projected, jnp.mean(full * full, axis=0), current)


def solution(mesh):
    in_specs = (
        P(("grp", "pan"), None),
        P("grp", None),
        P("grp", "pan"),
        P(None, "grp", "pan"),
        P("grp"),
    )
    out_specs = (P("grp", "pan"), P(("grp", "pan")), P("grp", "pan"))
    return jax.shard_map(body, mesh=mesh, in_specs=in_specs, out_specs=out_specs, check_vma=False)
```

```python
from functools import partial

import jax
import jax.numpy as jnp
from jax import lax
from jax.experimental import pallas as pl
from jax.experimental.pallas import tpu as pltpu
from jax.sharding import PartitionSpec as P

UNITS = 32
TILE = 128
SHARE = 1
HBM = pl.BlockSpec(memory_space=pltpu.HBM)


def plan(bits, width):
    if width < 256:
        return [16, 16], 2, "MMFFP"
    near = {0: 0, 1: 2, 2: 2}
    first, second = near.get(bits[0], 4), near.get(bits[1], 4)
    if second == 0:
        return [12, 10, 7, 3], 2, "MMFMFPMFFP"
    if first == 0:
        return [8] * 4, 2, "MMMFMFFPFP"
    if first > second and bits[1] == 1:
        return [7, 6, 5, 5, 4, 3, 2], 2, "MMFMFMFMFMFPMFFP"
    if first > second:
        return [5, 5, 4, 4, 4, 4, 3, 3], 2, "MMFMFMFMFMFMFPMFFP"
    if first < second:
        return [4] * 8, 2, "MMMFMFMFMFMFMFFPFP"
    return [4] * 8, 2, "MM" + "FM" * 6 + "FPFP"


def gather_order(bits, bit_count):
    top = bit_count - 1
    if bits[0]:
        return list(dict.fromkeys([bits[0], *reversed(range(bit_count))])), bit_count
    return list(dict.fromkeys([top, bits[1], *reversed(range(bit_count))])), 2 if bits[1] < top else 3


def swapped(x, bit):
    return lax.ppermute(x, "pan", [(i, i ^ 1 << bit) for i in range(lax.axis_size("pan"))])


def after(x, *earlier):
    return lax.optimization_barrier((x, *earlier))[0]


def in_device_order(values, places):
    me, count = lax.axis_index("pan"), lax.axis_size("pan")
    picked = values.shape[0] // count
    away = jnp.arange(count, dtype=jnp.int32) ^ me
    block = jnp.zeros_like(away)
    for bit in range(count.bit_length() - 1):
        block = block + (((away >> bit) & 1) << places[bit])
    rows = (block[:, None] * picked + jnp.arange(picked, dtype=jnp.int32)).reshape(-1)
    pick = rows[:, None] == jnp.arange(values.shape[0], dtype=jnp.int32)[None, :]
    return jnp.dot(pick.astype(values.dtype), values, preferred_element_type=jnp.float32).astype(values.dtype)


def cost(rows, width, columns):
    return pl.CostEstimate(
        flops=rows * width * columns * 2 * SHARE, bytes_accessed=rows * (width + columns) * 2 * SHARE, transcendentals=0
    )


def rotate(own, own_start, other, rotations, step, whole=None, start=0, depth=None):
    rows, width = other.shape
    tiles = rows // TILE

    def kernel(own_ref, other_ref, maps_ref, *rest):
        fresh_ref, own_held, other_held, map_held, fresh_held, map_sem, in_sems, out_sem = rest[-8:]

        def arrivals(i):
            at = pl.ds(pl.multiple_of(i * TILE, TILE), TILE)
            source = pl.ds(pl.multiple_of(own_start + i * TILE, TILE), TILE)
            return [
                pltpu.make_async_copy(own_ref.at[source], own_held.at[at], in_sems.at[0, i]),
                pltpu.make_async_copy(other_ref.at[at], other_held.at[at], in_sems.at[1, i]),
            ]

        def fetch(i, carry):
            for copy in arrivals(i):
                copy.start()
            return carry

        def tile(i, carry):
            for copy in arrivals(i):
                copy.wait()
            at = pl.ds(pl.multiple_of(i * TILE, TILE), TILE)
            target = pl.ds(pl.multiple_of(start + i * TILE, TILE), TILE)
            pair = jnp.concatenate([own_held[at], other_held[at]], axis=1)
            fresh = jnp.dot(pair, map_held[...], preferred_element_type=jnp.float32)
            fresh_held[at] = fresh.astype(jnp.bfloat16)
            pltpu.make_async_copy(fresh_held.at[at], fresh_ref.at[target], out_sem).start()
            return carry

        map_copy = pltpu.make_async_copy(maps_ref.at[step], map_held, map_sem)
        map_copy.start()
        lax.fori_loop(0, tiles, fetch, 0)
        map_copy.wait()
        lax.fori_loop(0, tiles, tile, 0)
        pltpu.make_async_copy(fresh_held, fresh_ref.at[pl.ds(start, rows)], out_sem).wait()

    args = [own, other, rotations] + [whole] * (whole is not None)
    return pl.pallas_call(
        kernel,
        in_specs=[HBM] * len(args),
        out_specs=HBM,
        out_shape=jax.ShapeDtypeStruct((depth or rows, width), jnp.bfloat16),
        scratch_shapes=[
            pltpu.VMEM((rows, width), jnp.bfloat16),
            pltpu.VMEM((rows, width), jnp.bfloat16),
            pltpu.VMEM((2 * width, width), jnp.bfloat16),
            pltpu.VMEM((rows, width), jnp.bfloat16),
            pltpu.SemaphoreType.DMA,
            pltpu.SemaphoreType.DMA((2, tiles)),
            pltpu.SemaphoreType.DMA,
        ],
        input_output_aliases={} if whole is None else {3: 0},
        compiler_params=pltpu.CompilerParams(vmem_limit_bytes=60 << 20),
        cost_estimate=cost(rows, 2 * width, width),
    )(*args)


def project(samples, basis, start, rows, full=None):
    width = basis.shape[1]
    count = samples.shape[0]
    tile = min(1024, rows)
    depth = min(512, tile)
    first = start // tile

    def kernel(samples_ref, basis_ref, *rest):
        sum_ref = rest[-1]

        @pl.when(pl.program_id(0) == 0)
        def _():
            sum_ref[...] = jnp.zeros_like(sum_ref) if full is None else rest[0][...]

        def part(j, carry):
            at = pl.ds(pl.multiple_of(j * depth, depth), depth)
            sum_ref[...] += jnp.dot(samples_ref[:, at], basis_ref[at], preferred_element_type=jnp.float32)
            return carry

        lax.fori_loop(0, tile // depth, part, 0)

    held = pl.BlockSpec((count, width), lambda i: (0, 0))
    return pl.pallas_call(
        kernel,
        grid=(rows // tile,),
        in_specs=[
            pl.BlockSpec((count, tile), lambda i: (0, first + i)),
            pl.BlockSpec((tile, width), lambda i: (first + i, 0)),
        ]
        + [held] * (full is not None),
        out_specs=held,
        out_shape=jax.ShapeDtypeStruct((count, width), jnp.float32),
        compiler_params=pltpu.CompilerParams(vmem_limit_bytes=60 << 20),
        cost_estimate=cost(count, rows, width),
    )(*([samples, basis] + [full] * (full is not None)))


def joined(upper, lower):
    count = upper.shape[0]

    def kernel(upper_ref, lower_ref, whole_ref, sems):
        copies = [
            pltpu.make_async_copy(upper_ref, whole_ref.at[:count], sems.at[0]),
            pltpu.make_async_copy(lower_ref, whole_ref.at[count:], sems.at[1]),
        ]
        for copy in copies:
            copy.start()
        for copy in copies:
            copy.wait()

    return pl.pallas_call(
        kernel,
        in_specs=[HBM, HBM],
        out_specs=pl.BlockSpec(memory_space=pltpu.VMEM),
        out_shape=jax.ShapeDtypeStruct((2 * count, *upper.shape[1:]), upper.dtype),
        scratch_shapes=[pltpu.SemaphoreType.DMA((2,))],
        compiler_params=pltpu.CompilerParams(vmem_limit_bytes=60 << 20),
        cost_estimate=pl.CostEstimate(flops=0, bytes_accessed=8 * upper.size, transcendentals=0),
    )(upper, lower)


def refresh(own, basis, rotations, bits):
    depth, width = basis.shape
    units, window, order = plan(bits, width)
    sizes = [part * depth // UNITS for part in units]
    starts = [sum(sizes[:i]) for i in range(len(sizes))]
    chunks = len(sizes)

    def send(chunk, *earlier):
        return swapped(after(basis, *earlier)[starts[chunk] : starts[chunk] + sizes[chunk]], bits[0])

    gather, soon = gather_order(bits, lax.axis_size("pan").bit_length() - 1)
    samples = joined(own[None], swapped(own[None], gather[0]))
    parts = [basis[starts[chunk] : starts[chunk] + sizes[chunk]] for chunk in range(min(window, chunks))]
    arriving = [swapped(after(part, samples), bits[0]) for part in parts]
    for bit in gather[1:soon]:
        samples = joined(samples, swapped(samples, bit))
    middles, coming = [], []
    basis_out = full = None
    done = projected = 0
    earlier = (samples,)
    for kind in order:
        if kind == "M":
            chunk = len(middles)
            fresh = rotate(after(basis, *earlier), starts[chunk], arriving[chunk], rotations, 0)
            middles.append(fresh)
            coming.append(swapped(fresh, bits[1]))
            if chunk + window < chunks:
                arriving.append(send(chunk + window, fresh))
            earlier = (fresh,)
        elif kind == "F":
            if not done:
                for bit in gather[soon:]:
                    samples = joined(samples, swapped(after(samples, *earlier), bit))
                    earlier = (samples,)
                samples = samples.reshape(-1, samples.shape[-1])
            basis_out = rotate(after(middles[done], *earlier), 0, coming[done], rotations, 1, basis_out, starts[done], depth)
            done += 1
            earlier = (basis_out,)
        else:
            end = starts[done] // 1024 * 1024 if done < chunks else depth
            full = project(after(samples, *earlier), basis_out, projected, end - projected, full)
            projected = end
            earlier = (full,)
    return full, basis_out


def body(pool_grads, sample_idx, basis, rotations, jacobi_bits):
    bit_count = lax.axis_size("pan").bit_length() - 1
    own = jnp.take(pool_grads, sample_idx[lax.axis_index("pan")], axis=0)
    pairs = [(a, b) for a in range(bit_count) for b in range(bit_count) if a != b]
    first, second = jacobi_bits[0], jacobi_bits[1]
    branch = first * (bit_count - 1) + second - (second > first).astype(jnp.int32)
    orders = [gather_order(pair, bit_count)[0] for pair in pairs]
    places = jnp.array([[order.index(bit) for bit in range(bit_count)] for order in orders], jnp.int32)[branch]
    full, current = lax.switch(branch, [partial(refresh, bits=pair) for pair in pairs], own, basis, rotations)
    projected = in_device_order(full.astype(jnp.bfloat16), places)
    return (projected, jnp.mean(full * full, axis=0), current)


def solution(mesh):
    in_specs = (
        P(("grp", "pan"), None),
        P("grp", None),
        P("grp", "pan"),
        P(None, "grp", "pan"),
        P("grp"),
    )
    out_specs = (P("grp", "pan"), P(("grp", "pan")), P("grp", "pan"))
    return jax.shard_map(body, mesh=mesh, in_specs=in_specs, out_specs=out_specs, check_vma=False)
```

```python
from functools import partial

import jax
import jax.numpy as jnp
from jax import lax
from jax.experimental import pallas as pl
from jax.experimental.pallas import tpu as pltpu
from jax.sharding import PartitionSpec as P

UNITS = 32
TILE = 128
SHARE = 1
HBM = pl.BlockSpec(memory_space=pltpu.HBM)


def plan(bits, width):
    if width < 256:
        return [16, 16], 2, "MMFFP"
    near = {0: 0, 1: 2, 2: 2}
    first, second = near.get(bits[0], 4), near.get(bits[1], 4)
    if second == 0:
        return [12, 10, 7, 3], 2, "MMFMFPMFFP"
    if first == 0:
        return [8] * 4, 2, "MMMFMFFPFP"
    if first > second and bits[1] == 1:
        return [7, 6, 5, 5, 4, 3, 2], 2, "MMFMFMFMFMFPMFFP"
    if first > second:
        return [4] * 8, 2, "MMFMFMFMFMFMFPMFFP"
    if first < second:
        return [4] * 8, 2, "MMMFMFMFMFMFMFFPFP"
    return [4] * 8, 2, "MM" + "FM" * 6 + "FPFP"


def gather_order(bits, bit_count):
    top = bit_count - 1
    if bits[0]:
        return list(dict.fromkeys([top, bits[0], *reversed(range(bit_count))])), bit_count
    return list(dict.fromkeys([top, bits[1], *reversed(range(bit_count))])), 2 if bits[1] < top else 3


def swapped(x, bit):
    return lax.ppermute(x, "pan", [(i, i ^ 1 << bit) for i in range(lax.axis_size("pan"))])


def after(x, *earlier):
    return lax.optimization_barrier((x, *earlier))[0]


def cost(rows, width, columns):
    return pl.CostEstimate(
        flops=rows * width * columns * 2 * SHARE, bytes_accessed=rows * (width + columns) * 2 * SHARE, transcendentals=0
    )


def rotate(own, own_start, other, rotations, step, whole=None, start=0, depth=None):
    rows, width = other.shape
    tiles = rows // TILE

    def kernel(own_ref, other_ref, maps_ref, *rest):
        fresh_ref, own_held, other_held, map_held, fresh_held, map_sem, in_sems, out_sem = rest[-8:]

        def arrivals(i):
            at = pl.ds(pl.multiple_of(i * TILE, TILE), TILE)
            source = pl.ds(pl.multiple_of(own_start + i * TILE, TILE), TILE)
            return [
                pltpu.make_async_copy(own_ref.at[source], own_held.at[at], in_sems.at[0, i]),
                pltpu.make_async_copy(other_ref.at[at], other_held.at[at], in_sems.at[1, i]),
            ]

        def fetch(i, carry):
            for copy in arrivals(i):
                copy.start()
            return carry

        def tile(i, carry):
            for copy in arrivals(i):
                copy.wait()
            at = pl.ds(pl.multiple_of(i * TILE, TILE), TILE)
            target = pl.ds(pl.multiple_of(start + i * TILE, TILE), TILE)
            pair = jnp.concatenate([own_held[at], other_held[at]], axis=1)
            fresh = jnp.dot(pair, map_held[...], preferred_element_type=jnp.float32)
            fresh_held[at] = fresh.astype(jnp.bfloat16)
            pltpu.make_async_copy(fresh_held.at[at], fresh_ref.at[target], out_sem).start()
            return carry

        map_copy = pltpu.make_async_copy(maps_ref.at[step], map_held, map_sem)
        map_copy.start()
        lax.fori_loop(0, tiles, fetch, 0)
        map_copy.wait()
        lax.fori_loop(0, tiles, tile, 0)
        pltpu.make_async_copy(fresh_held, fresh_ref.at[pl.ds(start, rows)], out_sem).wait()

    args = [own, other, rotations] + [whole] * (whole is not None)
    return pl.pallas_call(
        kernel,
        in_specs=[HBM] * len(args),
        out_specs=HBM,
        out_shape=jax.ShapeDtypeStruct((depth or rows, width), jnp.bfloat16),
        scratch_shapes=[
            pltpu.VMEM((rows, width), jnp.bfloat16),
            pltpu.VMEM((rows, width), jnp.bfloat16),
            pltpu.VMEM((2 * width, width), jnp.bfloat16),
            pltpu.VMEM((rows, width), jnp.bfloat16),
            pltpu.SemaphoreType.DMA,
            pltpu.SemaphoreType.DMA((2, tiles)),
            pltpu.SemaphoreType.DMA,
        ],
        input_output_aliases={} if whole is None else {3: 0},
        compiler_params=pltpu.CompilerParams(vmem_limit_bytes=60 << 20),
        cost_estimate=cost(rows, 2 * width, width),
    )(*args)


def project(samples, basis, start, rows, full=None, gather=None):
    width = basis.shape[1]
    count = samples.shape[0]
    tile = min(1024, rows)
    depth = min(512, tile)
    first = start // tile

    def kernel(samples_ref, basis_ref, *rest):
        sum_ref = rest[-1]

        @pl.when(pl.program_id(0) == 0)
        def _():
            sum_ref[...] = jnp.zeros_like(sum_ref) if full is None else rest[0][...]

        def part(j, carry):
            at = pl.ds(pl.multiple_of(j * depth, depth), depth)
            sum_ref[...] += jnp.dot(samples_ref[:, at], basis_ref[at], preferred_element_type=jnp.float32)
            return carry

        lax.fori_loop(0, tile // depth, part, 0)
        if gather is not None:
            projected_ref, scalings_ref = rest[-3:-1]

            @pl.when(pl.program_id(0) == rows // tile - 1)
            def _():
                picked = count >> len(gather)
                row = lax.broadcasted_iota(jnp.int32, (count, count), 0)
                column = lax.broadcasted_iota(jnp.int32, (count, count), 1)
                source = jnp.zeros_like(column) + lax.axis_index("pan")
                for step, bit in enumerate(gather):
                    source = source ^ (((column // (picked << step)) & 1) << bit)
                pick = (row == source * picked + column % picked).astype(jnp.float32).astype(jnp.bfloat16)
                total = sum_ref[...]
                ordered = jnp.dot(pick, total.astype(jnp.bfloat16), preferred_element_type=jnp.float32)
                projected_ref[...] = ordered.astype(jnp.bfloat16)
                scalings_ref[...] = jnp.sum(total * total, axis=0, keepdims=True) / count

    held = pl.BlockSpec((count, width), lambda i: (0, 0))
    sums = jax.ShapeDtypeStruct((count, width), jnp.float32)
    out_specs, out_shape, scratch = held, sums, []
    if gather is not None:
        out_specs = [held, pl.BlockSpec((1, width), lambda i: (0, 0))]
        out_shape = [jax.ShapeDtypeStruct((count, width), jnp.bfloat16), jax.ShapeDtypeStruct((1, width), jnp.float32)]
        scratch = [pltpu.VMEM((count, width), jnp.float32)]
    return pl.pallas_call(
        kernel,
        grid=(rows // tile,),
        in_specs=[
            pl.BlockSpec((count, tile), lambda i: (0, first + i)),
            pl.BlockSpec((tile, width), lambda i: (first + i, 0)),
        ]
        + [held] * (full is not None),
        out_specs=out_specs,
        out_shape=out_shape,
        scratch_shapes=scratch,
        compiler_params=pltpu.CompilerParams(vmem_limit_bytes=60 << 20),
        cost_estimate=cost(count, rows, width),
    )(*([samples, basis] + [full] * (full is not None)))


def joined(upper, lower):
    count = upper.shape[0]

    def kernel(upper_ref, lower_ref, whole_ref, sems):
        copies = [
            pltpu.make_async_copy(upper_ref, whole_ref.at[:count], sems.at[0]),
            pltpu.make_async_copy(lower_ref, whole_ref.at[count:], sems.at[1]),
        ]
        for copy in copies:
            copy.start()
        for copy in copies:
            copy.wait()

    return pl.pallas_call(
        kernel,
        in_specs=[HBM, HBM],
        out_specs=pl.BlockSpec(memory_space=pltpu.VMEM),
        out_shape=jax.ShapeDtypeStruct((2 * count, *upper.shape[1:]), upper.dtype),
        scratch_shapes=[pltpu.SemaphoreType.DMA((2,))],
        compiler_params=pltpu.CompilerParams(vmem_limit_bytes=60 << 20),
        cost_estimate=pl.CostEstimate(flops=0, bytes_accessed=8 * upper.size, transcendentals=0),
    )(upper, lower)


def refresh(own, sent, basis, rotations, bits):
    depth, width = basis.shape
    units, window, order = plan(bits, width)
    sizes = [part * depth // UNITS for part in units]
    starts = [sum(sizes[:i]) for i in range(len(sizes))]
    chunks = len(sizes)

    def send(chunk, *earlier):
        return swapped(after(basis, *earlier)[starts[chunk] : starts[chunk] + sizes[chunk]], bits[0])

    gather, soon = gather_order(bits, lax.axis_size("pan").bit_length() - 1)
    ahead = 2 if gather[1] == bits[0] else 1
    samples = joined(own, sent)
    for bit in gather[1:ahead]:
        samples = joined(samples, swapped(samples, bit))
    parts = [basis[starts[chunk] : starts[chunk] + sizes[chunk]] for chunk in range(min(window, chunks))]
    if ahead > 1:
        parts = [after(part, samples) for part in parts]
    arriving = [swapped(part, bits[0]) for part in parts]
    for bit in gather[ahead:soon]:
        samples = joined(samples, swapped(samples, bit))
    middles, coming = [], []
    basis_out = full = None
    done = projected = 0
    earlier = (samples,)
    for kind in order:
        if kind == "M":
            chunk = len(middles)
            fresh = rotate(after(basis, *earlier), starts[chunk], arriving[chunk], rotations, 0)
            middles.append(fresh)
            coming.append(swapped(fresh, bits[1]))
            if chunk + window < chunks:
                arriving.append(send(chunk + window, fresh))
            earlier = (fresh,)
        elif kind == "F":
            if not done:
                for bit in gather[soon:]:
                    samples = joined(samples, swapped(after(samples, *earlier), bit))
                    earlier = (samples,)
                samples = samples.reshape(-1, samples.shape[-1])
            basis_out = rotate(after(middles[done], *earlier), 0, coming[done], rotations, 1, basis_out, starts[done], depth)
            done += 1
            earlier = (basis_out,)
        else:
            end = starts[done] // 1024 * 1024 if done < chunks else depth
            last = gather if end == depth else None
            full = project(after(samples, *earlier), basis_out, projected, end - projected, full, last)
            projected = end
            earlier = (full,)
    return (*full, basis_out)


def body(pool_grads, sample_idx, basis, rotations, jacobi_bits):
    bit_count = lax.axis_size("pan").bit_length() - 1
    own = jnp.take(pool_grads, sample_idx[lax.axis_index("pan")], axis=0)[None]
    pairs = [(a, b) for a in reversed(range(bit_count)) for b in reversed(range(bit_count)) if a != b]
    first, second = bit_count - 1 - jacobi_bits[0], bit_count - 1 - jacobi_bits[1]
    branch = first * (bit_count - 1) + second - (second > first).astype(jnp.int32)
    branches = [partial(refresh, bits=pair) for pair in pairs]
    projected, scalings, current = lax.switch(branch, branches, own, swapped(own, bit_count - 1), basis, rotations)
    return projected, scalings.reshape(-1), current


def solution(mesh):
    in_specs = (
        P(("grp", "pan"), None),
        P("grp", None),
        P("grp", "pan"),
        P(None, "grp", "pan"),
        P("grp"),
    )
    out_specs = (P("grp", "pan"), P(("grp", "pan")), P("grp", "pan"))
    return jax.shard_map(body, mesh=mesh, in_specs=in_specs, out_specs=out_specs, check_vma=False)
```

```python
from functools import partial

import jax
import jax.numpy as jnp
from jax import lax
from jax.experimental import pallas as pl
from jax.experimental.pallas import tpu as pltpu
from jax.sharding import PartitionSpec as P

UNITS = 32
TILE = 128
SHARE = 1
HBM = pl.BlockSpec(memory_space=pltpu.HBM)


def plan(bits, width):
    if width < 256:
        return [16, 16], 2, "MMFFP"
    near = {0: 0, 1: 2, 2: 2}
    first, second = near.get(bits[0], 4), near.get(bits[1], 4)
    if second == 0:
        return [12, 10, 7, 3], 2, "MMFMFPMFFP"
    if first == 0:
        return [8] * 4, 2, "MMMFMFFPFP"
    if first > second and bits[1] == 1:
        return [7, 6, 5, 5, 4, 3, 2], 2, "MMFMFMFMFPMFMFFP"
    if first > second:
        return [4] * 8, 2, "MMFMFMFMFMFMFPMFFP"
    return [4] * 8, 2, "MM" + "FM" * 6 + "FPFP"


def gather_order(bits, bit_count):
    top = bit_count - 1
    if bits[0]:
        return list(dict.fromkeys([top, bits[0], *reversed(range(bit_count))])), bit_count
    return list(dict.fromkeys([top, bits[1], *reversed(range(bit_count))])), 2 if bits[1] < top else 3


def swapped(x, bit):
    return lax.ppermute(x, "pan", [(i, i ^ 1 << bit) for i in range(lax.axis_size("pan"))])


def after(x, *earlier):
    return lax.optimization_barrier((x, *earlier))[0]


def cost(rows, width, columns):
    return pl.CostEstimate(
        flops=rows * width * columns * 2 * SHARE, bytes_accessed=rows * (width + columns) * 2 * SHARE, transcendentals=0
    )


def rotate(own, own_start, other, rotations, step, whole=None, start=0, depth=None):
    rows, width = other.shape
    tiles = rows // TILE

    def kernel(own_ref, other_ref, maps_ref, *rest):
        fresh_ref, own_held, other_held, map_held, fresh_held, map_sem, in_sems, out_sem = rest[-8:]

        def arrivals(i):
            at = pl.ds(pl.multiple_of(i * TILE, TILE), TILE)
            source = pl.ds(pl.multiple_of(own_start + i * TILE, TILE), TILE)
            return [
                pltpu.make_async_copy(own_ref.at[source], own_held.at[at], in_sems.at[0, i]),
                pltpu.make_async_copy(other_ref.at[at], other_held.at[at], in_sems.at[1, i]),
            ]

        def fetch(i, carry):
            for copy in arrivals(i):
                copy.start()
            return carry

        def tile(i, carry):
            for copy in arrivals(i):
                copy.wait()
            at = pl.ds(pl.multiple_of(i * TILE, TILE), TILE)
            target = pl.ds(pl.multiple_of(start + i * TILE, TILE), TILE)
            pair = jnp.concatenate([own_held[at], other_held[at]], axis=1)
            fresh = jnp.dot(pair, map_held[...], preferred_element_type=jnp.float32)
            fresh_held[at] = fresh.astype(jnp.bfloat16)
            pltpu.make_async_copy(fresh_held.at[at], fresh_ref.at[target], out_sem).start()
            return carry

        map_copy = pltpu.make_async_copy(maps_ref.at[step], map_held, map_sem)
        map_copy.start()
        lax.fori_loop(0, tiles, fetch, 0)
        map_copy.wait()
        lax.fori_loop(0, tiles, tile, 0)
        pltpu.make_async_copy(fresh_held, fresh_ref.at[pl.ds(start, rows)], out_sem).wait()

    args = [own, other, rotations] + [whole] * (whole is not None)
    return pl.pallas_call(
        kernel,
        in_specs=[HBM] * len(args),
        out_specs=HBM,
        out_shape=jax.ShapeDtypeStruct((depth or rows, width), jnp.bfloat16),
        scratch_shapes=[
            pltpu.VMEM((rows, width), jnp.bfloat16),
            pltpu.VMEM((rows, width), jnp.bfloat16),
            pltpu.VMEM((2 * width, width), jnp.bfloat16),
            pltpu.VMEM((rows, width), jnp.bfloat16),
            pltpu.SemaphoreType.DMA,
            pltpu.SemaphoreType.DMA((2, tiles)),
            pltpu.SemaphoreType.DMA,
        ],
        input_output_aliases={} if whole is None else {3: 0},
        compiler_params=pltpu.CompilerParams(vmem_limit_bytes=60 << 20),
        cost_estimate=cost(rows, 2 * width, width),
    )(*args)


def project(samples, basis, start, rows, full=None, gather=None):
    width = basis.shape[1]
    count = samples.shape[0]
    tile = min(1024, rows)
    depth = min(512, tile)
    first = start // tile

    def kernel(samples_ref, basis_ref, *rest):
        sum_ref = rest[-1]

        @pl.when(pl.program_id(0) == 0)
        def _():
            sum_ref[...] = jnp.zeros_like(sum_ref) if full is None else rest[0][...]

        def part(j, carry):
            at = pl.ds(pl.multiple_of(j * depth, depth), depth)
            sum_ref[...] += jnp.dot(samples_ref[:, at], basis_ref[at], preferred_element_type=jnp.float32)
            return carry

        lax.fori_loop(0, tile // depth, part, 0)
        if gather is not None:
            projected_ref, scalings_ref = rest[-3:-1]

            @pl.when(pl.program_id(0) == rows // tile - 1)
            def _():
                picked = count >> len(gather)
                row = lax.broadcasted_iota(jnp.int32, (count, count), 0)
                column = lax.broadcasted_iota(jnp.int32, (count, count), 1)
                source = jnp.zeros_like(column) + lax.axis_index("pan")
                for step, bit in enumerate(gather):
                    source = source ^ (((column // (picked << step)) & 1) << bit)
                pick = (row == source * picked + column % picked).astype(jnp.float32).astype(jnp.bfloat16)
                total = sum_ref[...]
                ordered = jnp.dot(pick, total.astype(jnp.bfloat16), preferred_element_type=jnp.float32)
                projected_ref[...] = ordered.astype(jnp.bfloat16)
                scalings_ref[...] = jnp.sum(total * total, axis=0, keepdims=True) / count

    held = pl.BlockSpec((count, width), lambda i: (0, 0))
    sums = jax.ShapeDtypeStruct((count, width), jnp.float32)
    out_specs, out_shape, scratch = held, sums, []
    if gather is not None:
        out_specs = [held, pl.BlockSpec((1, width), lambda i: (0, 0))]
        out_shape = [jax.ShapeDtypeStruct((count, width), jnp.bfloat16), jax.ShapeDtypeStruct((1, width), jnp.float32)]
        scratch = [pltpu.VMEM((count, width), jnp.float32)]
    return pl.pallas_call(
        kernel,
        grid=(rows // tile,),
        in_specs=[
            pl.BlockSpec((count, tile), lambda i: (0, first + i)),
            pl.BlockSpec((tile, width), lambda i: (first + i, 0)),
        ]
        + [held] * (full is not None),
        out_specs=out_specs,
        out_shape=out_shape,
        scratch_shapes=scratch,
        compiler_params=pltpu.CompilerParams(vmem_limit_bytes=60 << 20),
        cost_estimate=cost(count, rows, width),
    )(*([samples, basis] + [full] * (full is not None)))


def joined(upper, lower):
    count = upper.shape[0]

    def kernel(upper_ref, lower_ref, whole_ref, sems):
        copies = [
            pltpu.make_async_copy(upper_ref, whole_ref.at[:count], sems.at[0]),
            pltpu.make_async_copy(lower_ref, whole_ref.at[count:], sems.at[1]),
        ]
        for copy in copies:
            copy.start()
        for copy in copies:
            copy.wait()

    return pl.pallas_call(
        kernel,
        in_specs=[HBM, HBM],
        out_specs=pl.BlockSpec(memory_space=pltpu.VMEM),
        out_shape=jax.ShapeDtypeStruct((2 * count, *upper.shape[1:]), upper.dtype),
        scratch_shapes=[pltpu.SemaphoreType.DMA((2,))],
        compiler_params=pltpu.CompilerParams(vmem_limit_bytes=60 << 20),
        cost_estimate=pl.CostEstimate(flops=0, bytes_accessed=8 * upper.size, transcendentals=0),
    )(upper, lower)


def refresh(own, sent, basis, rotations, bits):
    depth, width = basis.shape
    units, window, order = plan(bits, width)
    sizes = [part * depth // UNITS for part in units]
    starts = [sum(sizes[:i]) for i in range(len(sizes))]
    chunks = len(sizes)

    def send(chunk, *earlier):
        return swapped(after(basis, *earlier)[starts[chunk] : starts[chunk] + sizes[chunk]], bits[0])

    gather, soon = gather_order(bits, lax.axis_size("pan").bit_length() - 1)
    ahead = 2 if gather[1] == bits[0] else 1
    samples = joined(own, sent)
    for bit in gather[1:ahead]:
        samples = joined(samples, swapped(samples, bit))
    parts = [basis[starts[chunk] : starts[chunk] + sizes[chunk]] for chunk in range(min(window, chunks))]
    if ahead > 1:
        parts = [after(part, samples) for part in parts]
    arriving = [swapped(part, bits[0]) for part in parts]
    for bit in gather[ahead:soon]:
        samples = joined(samples, swapped(samples, bit))
    middles, coming = [], []
    basis_out = full = None
    done = projected = 0
    earlier = (samples,)
    for kind in order:
        if kind == "M":
            chunk = len(middles)
            fresh = rotate(after(basis, *earlier), starts[chunk], arriving[chunk], rotations, 0)
            middles.append(fresh)
            coming.append(swapped(fresh, bits[1]))
            if chunk + window < chunks:
                arriving.append(send(chunk + window, fresh))
            earlier = (fresh,)
        elif kind == "F":
            if not done:
                for bit in gather[soon:]:
                    samples = joined(samples, swapped(after(samples, *earlier), bit))
                    earlier = (samples,)
                samples = samples.reshape(-1, samples.shape[-1])
            basis_out = rotate(after(middles[done], *earlier), 0, coming[done], rotations, 1, basis_out, starts[done], depth)
            done += 1
            earlier = (basis_out,)
        else:
            end = starts[done] // 1024 * 1024 if done < chunks else depth
            last = gather if end == depth else None
            full = project(after(samples, *earlier), basis_out, projected, end - projected, full, last)
            projected = end
            earlier = (full,)
    return (*full, basis_out)


def body(pool_grads, sample_idx, basis, rotations, jacobi_bits):
    bit_count = lax.axis_size("pan").bit_length() - 1
    own = jnp.take(pool_grads, sample_idx[lax.axis_index("pan")], axis=0)[None]
    pairs = [(a, b) for a in reversed(range(bit_count)) for b in reversed(range(bit_count)) if a != b]
    first, second = bit_count - 1 - jacobi_bits[0], bit_count - 1 - jacobi_bits[1]
    branch = first * (bit_count - 1) + second - (second > first).astype(jnp.int32)
    branches = [partial(refresh, bits=pair) for pair in pairs]
    projected, scalings, current = lax.switch(branch, branches, own, swapped(own, bit_count - 1), basis, rotations)
    return projected, scalings.reshape(-1), current


def solution(mesh):
    in_specs = (
        P(("grp", "pan"), None),
        P("grp", None),
        P("grp", "pan"),
        P(None, "grp", "pan"),
        P("grp"),
    )
    out_specs = (P("grp", "pan"), P(("grp", "pan")), P("grp", "pan"))
    return jax.shard_map(body, mesh=mesh, in_specs=in_specs, out_specs=out_specs, check_vma=False)
```

```python
from functools import partial

import jax
import jax.numpy as jnp
from jax import lax
from jax.experimental import pallas as pl
from jax.experimental.pallas import tpu as pltpu
from jax.sharding import PartitionSpec as P

UNITS = 32
TILE = 128
SHARE = 1
HBM = pl.BlockSpec(memory_space=pltpu.HBM)


def plan(bits, width):
    if width < 256:
        return [16, 16], 2, "MMFFP"
    near = {0: 0, 1: 2, 2: 2}
    first, second = near.get(bits[0], 4), near.get(bits[1], 4)
    if second == 0:
        return [12, 10, 7, 3], 2, "MMFMFPMFFP"
    if first == 0:
        return [8] * 4, 2, "MMFMFMFPFP"
    if first > second and bits[1] == 1:
        return [7, 6, 5, 5, 4, 3, 2], 2, "MMFMFMFMFPMFMFFP"
    if first > second:
        return [4] * 8, 2, "MMFMFMFMFMFMFPMFFP"
    return [4] * 8, 2, "MM" + "FM" * 6 + "FPFP"


def gather_order(bits, bit_count):
    top = bit_count - 1
    if bits[0]:
        return list(dict.fromkeys([top, bits[0], *reversed(range(bit_count))])), bit_count
    return list(dict.fromkeys([top, bits[1], *reversed(range(bit_count))])), 2 if bits[1] < top else 3


def swapped(x, bit):
    return lax.ppermute(x, "pan", [(i, i ^ 1 << bit) for i in range(lax.axis_size("pan"))])


def after(x, *earlier):
    return lax.optimization_barrier((x, *earlier))[0]


def cost(rows, width, columns):
    return pl.CostEstimate(
        flops=rows * width * columns * 2 * SHARE, bytes_accessed=rows * (width + columns) * 2 * SHARE, transcendentals=0
    )


def rotate(own, own_start, other, rotations, step, whole=None, start=0, depth=None):
    rows, width = other.shape
    tiles = rows // TILE

    def kernel(own_ref, other_ref, maps_ref, *rest):
        fresh_ref, own_held, other_held, map_held, fresh_held, map_sem, in_sems, out_sem = rest[-8:]

        def arrivals(i):
            at = pl.ds(pl.multiple_of(i * TILE, TILE), TILE)
            source = pl.ds(pl.multiple_of(own_start + i * TILE, TILE), TILE)
            return [
                pltpu.make_async_copy(own_ref.at[source], own_held.at[at], in_sems.at[0, i]),
                pltpu.make_async_copy(other_ref.at[at], other_held.at[at], in_sems.at[1, i]),
            ]

        def fetch(i, carry):
            for copy in arrivals(i):
                copy.start()
            return carry

        def tile(i, carry):
            for copy in arrivals(i):
                copy.wait()
            at = pl.ds(pl.multiple_of(i * TILE, TILE), TILE)
            target = pl.ds(pl.multiple_of(start + i * TILE, TILE), TILE)
            pair = jnp.concatenate([own_held[at], other_held[at]], axis=1)
            fresh = jnp.dot(pair, map_held[...], preferred_element_type=jnp.float32)
            fresh_held[at] = fresh.astype(jnp.bfloat16)
            pltpu.make_async_copy(fresh_held.at[at], fresh_ref.at[target], out_sem).start()
            return carry

        map_copy = pltpu.make_async_copy(maps_ref.at[step], map_held, map_sem)
        map_copy.start()
        lax.fori_loop(0, tiles, fetch, 0)
        map_copy.wait()
        lax.fori_loop(0, tiles, tile, 0)
        pltpu.make_async_copy(fresh_held, fresh_ref.at[pl.ds(start, rows)], out_sem).wait()

    args = [own, other, rotations] + [whole] * (whole is not None)
    return pl.pallas_call(
        kernel,
        in_specs=[HBM] * len(args),
        out_specs=HBM,
        out_shape=jax.ShapeDtypeStruct((depth or rows, width), jnp.bfloat16),
        scratch_shapes=[
            pltpu.VMEM((rows, width), jnp.bfloat16),
            pltpu.VMEM((rows, width), jnp.bfloat16),
            pltpu.VMEM((2 * width, width), jnp.bfloat16),
            pltpu.VMEM((rows, width), jnp.bfloat16),
            pltpu.SemaphoreType.DMA,
            pltpu.SemaphoreType.DMA((2, tiles)),
            pltpu.SemaphoreType.DMA,
        ],
        input_output_aliases={} if whole is None else {3: 0},
        compiler_params=pltpu.CompilerParams(vmem_limit_bytes=60 << 20),
        cost_estimate=cost(rows, 2 * width, width),
    )(*args)


def project(samples, basis, start, rows, full=None, gather=None):
    width = basis.shape[1]
    count = samples.shape[0]
    tile = min(1024, rows)
    depth = min(512, tile)
    first = start // tile

    def kernel(samples_ref, basis_ref, *rest):
        sum_ref = rest[-1]

        @pl.when(pl.program_id(0) == 0)
        def _():
            sum_ref[...] = jnp.zeros_like(sum_ref) if full is None else rest[0][...]

        def part(j, carry):
            at = pl.ds(pl.multiple_of(j * depth, depth), depth)
            sum_ref[...] += jnp.dot(samples_ref[:, at], basis_ref[at], preferred_element_type=jnp.float32)
            return carry

        lax.fori_loop(0, tile // depth, part, 0)
        if gather is not None:
            projected_ref, scalings_ref = rest[-3:-1]

            @pl.when(pl.program_id(0) == rows // tile - 1)
            def _():
                picked = count >> len(gather)
                row = lax.broadcasted_iota(jnp.int32, (count, count), 0)
                column = lax.broadcasted_iota(jnp.int32, (count, count), 1)
                source = jnp.zeros_like(column) + lax.axis_index("pan")
                for step, bit in enumerate(gather):
                    source = source ^ (((column // (picked << step)) & 1) << bit)
                pick = (row == source * picked + column % picked).astype(jnp.float32).astype(jnp.bfloat16)
                total = sum_ref[...]
                ordered = jnp.dot(pick, total.astype(jnp.bfloat16), preferred_element_type=jnp.float32)
                projected_ref[...] = ordered.astype(jnp.bfloat16)
                scalings_ref[...] = jnp.sum(total * total, axis=0, keepdims=True) / count

    held = pl.BlockSpec((count, width), lambda i: (0, 0))
    sums = jax.ShapeDtypeStruct((count, width), jnp.float32)
    out_specs, out_shape, scratch = held, sums, []
    if gather is not None:
        out_specs = [held, pl.BlockSpec((1, width), lambda i: (0, 0))]
        out_shape = [jax.ShapeDtypeStruct((count, width), jnp.bfloat16), jax.ShapeDtypeStruct((1, width), jnp.float32)]
        scratch = [pltpu.VMEM((count, width), jnp.float32)]
    return pl.pallas_call(
        kernel,
        grid=(rows // tile,),
        in_specs=[
            pl.BlockSpec((count, tile), lambda i: (0, first + i)),
            pl.BlockSpec((tile, width), lambda i: (first + i, 0)),
        ]
        + [held] * (full is not None),
        out_specs=out_specs,
        out_shape=out_shape,
        scratch_shapes=scratch,
        compiler_params=pltpu.CompilerParams(vmem_limit_bytes=60 << 20),
        cost_estimate=cost(count, rows, width),
    )(*([samples, basis] + [full] * (full is not None)))


def joined(upper, lower):
    count = upper.shape[0]

    def kernel(upper_ref, lower_ref, whole_ref, sems):
        copies = [
            pltpu.make_async_copy(upper_ref, whole_ref.at[:count], sems.at[0]),
            pltpu.make_async_copy(lower_ref, whole_ref.at[count:], sems.at[1]),
        ]
        for copy in copies:
            copy.start()
        for copy in copies:
            copy.wait()

    return pl.pallas_call(
        kernel,
        in_specs=[HBM, HBM],
        out_specs=pl.BlockSpec(memory_space=pltpu.VMEM),
        out_shape=jax.ShapeDtypeStruct((2 * count, *upper.shape[1:]), upper.dtype),
        scratch_shapes=[pltpu.SemaphoreType.DMA((2,))],
        compiler_params=pltpu.CompilerParams(vmem_limit_bytes=60 << 20),
        cost_estimate=pl.CostEstimate(flops=0, bytes_accessed=8 * upper.size, transcendentals=0),
    )(upper, lower)


def refresh(own, sent, basis, rotations, bits):
    depth, width = basis.shape
    units, window, order = plan(bits, width)
    sizes = [part * depth // UNITS for part in units]
    starts = [sum(sizes[:i]) for i in range(len(sizes))]
    chunks = len(sizes)

    def send(chunk, *earlier):
        return swapped(after(basis, *earlier)[starts[chunk] : starts[chunk] + sizes[chunk]], bits[0])

    gather, soon = gather_order(bits, lax.axis_size("pan").bit_length() - 1)
    ahead = 2 if gather[1] == bits[0] else 1
    samples = joined(own, sent)
    for bit in gather[1:ahead]:
        samples = joined(samples, swapped(samples, bit))
    parts = [basis[starts[chunk] : starts[chunk] + sizes[chunk]] for chunk in range(min(window, chunks))]
    if ahead > 1:
        parts = [after(part, samples) for part in parts]
    arriving = [swapped(part, bits[0]) for part in parts]
    for bit in gather[ahead:soon]:
        samples = joined(samples, swapped(samples, bit))
    middles, coming = [], []
    basis_out = full = None
    done = projected = 0
    earlier = (samples,)
    for kind in order:
        if kind == "M":
            chunk = len(middles)
            fresh = rotate(after(basis, *earlier), starts[chunk], arriving[chunk], rotations, 0)
            middles.append(fresh)
            coming.append(swapped(fresh, bits[1]))
            if chunk + window < chunks:
                arriving.append(send(chunk + window, fresh))
            earlier = (fresh,)
        elif kind == "F":
            if not done:
                for bit in gather[soon:]:
                    samples = joined(samples, swapped(after(samples, *earlier), bit))
                    earlier = (samples,)
                samples = samples.reshape(-1, samples.shape[-1])
            basis_out = rotate(after(middles[done], *earlier), 0, coming[done], rotations, 1, basis_out, starts[done], depth)
            done += 1
            earlier = (basis_out,)
        else:
            end = starts[done] // 1024 * 1024 if done < chunks else depth
            last = gather if end == depth else None
            full = project(after(samples, *earlier), basis_out, projected, end - projected, full, last)
            projected = end
            earlier = (full,)
    return (*full, basis_out)


def body(pool_grads, sample_idx, basis, rotations, jacobi_bits):
    bit_count = lax.axis_size("pan").bit_length() - 1
    own = jnp.take(pool_grads, sample_idx[lax.axis_index("pan")], axis=0)[None]
    pairs = [(a, b) for a in reversed(range(bit_count)) for b in reversed(range(bit_count)) if a != b]
    first, second = bit_count - 1 - jacobi_bits[0], bit_count - 1 - jacobi_bits[1]
    branch = first * (bit_count - 1) + second - (second > first).astype(jnp.int32)
    branches = [partial(refresh, bits=pair) for pair in pairs]
    projected, scalings, current = lax.switch(branch, branches, own, swapped(own, bit_count - 1), basis, rotations)
    return projected, scalings.reshape(-1), current


def solution(mesh):
    in_specs = (
        P(("grp", "pan"), None),
        P("grp", None),
        P("grp", "pan"),
        P(None, "grp", "pan"),
        P("grp"),
    )
    out_specs = (P("grp", "pan"), P(("grp", "pan")), P("grp", "pan"))
    return jax.shard_map(body, mesh=mesh, in_specs=in_specs, out_specs=out_specs, check_vma=False)
```
